32 devices in a mesh: dp: 16 (over z, y, core), tensor: 2 (over x).
Axes of the slice: x: 2, y: 2, z: 4, core: 2. Of those that a mesh axis runs over, the one named last changes fastest.
Arguments:
- block_in: bfloat16 [32, 512, 1536], P('dp'), may hold values from -6 to 6
- cotangent: bfloat16 [32, 512, 1536], P('dp'), may hold values from -6 to 6
- segment_ids: int32 [32, 512], P('dp'), may hold values from 0 to 3, as said below
- positions: int32 [32, 512], P('dp'), may hold values from 0 to 2047, as said below
- norm1_gain: bfloat16 [1536], P('dp'), may hold values from 0.5 to 1.5
- norm2_gain: bfloat16 [1536], P('dp'), may hold values from 0.5 to 1.5
- w_query: bfloat16 [1536, 1536], P('dp', 'tensor'), may hold values from -0.15625 to 0.15625
- key_projection: bfloat16 [1536, 768], P('dp', 'tensor'), may hold values from -0.15625 to 0.15625
- value_projection: bfloat16 [1536, 768], P('dp', 'tensor'), may hold values from -0.15625 to 0.15625
- w_out: bfloat16 [1536, 1536], P('tensor', 'dp'), may hold values from -0.625 to 0.625
- w_gate: bfloat16 [1536, 4096], P('dp', 'tensor'), may hold values from -0.15625 to 0.15625
- w_up: bfloat16 [1536, 4096], P('dp', 'tensor'), may hold values from -0.15625 to 0.15625
- w_down: bfloat16 [4096, 1536], P('tensor', 'dp'), may hold values from -0.09375 to 0.09375
Outputs:
- block_out: bfloat16 [32, 512, 1536], P('dp')
- input_grad: float32 [32, 512, 1536], P('dp')
- norm1_grad: float32 [1536], P('dp')
- norm2_grad: float32 [1536], P('dp')
- query_grad: float32 [1536, 1536], P('dp', 'tensor')
- key_grad: float32 [1536, 768], P('dp', 'tensor')
- value_grad: float32 [1536, 768], P('dp', 'tensor')
- out_grad: float32 [1536, 1536], P('tensor', 'dp')
- gate_grad: float32 [1536, 4096], P('dp', 'tensor')
- up_grad: float32 [1536, 4096], P('dp', 'tensor')
- down_grad: float32 [4096, 1536], P('tensor', 'dp')
The draws below stay inside these ranges and needn't reach their ends.
Inputs may be any that keep to these rules, and one draw needn't show every extreme that they name: `segment_ids`: segment numbers of a sequence start at 0 and never fall; documents may continue from the previous sequence. Within a segment positions rise by one from token to token; a segment that starts a sequence may begin above 0.
All inputs are finite; a program needn't handle non-finite values.
Results may differ from the reference program's by a relative error of at most 0.015.
Values may be sent and summed in bfloat16 or wider, within the bound.
No kernel may reach another device: no remote copies, remote signals or barrier semaphores. Data moves between devices by JAX's collectives and lax.ppermute only.
A program may use at most 256 MiB of HBM per device.

```python
import math
import jax
import jax.numpy as jnp
from jax import lax

MODEL_WIDTH = 1536
NH = 16
KEY_VALUE_HEADS = 8
HEAD_SIZE = 96
FF = 4096
SEQ_LEN = 512
SEQ_DEV = 2
SEQS = 32


def packing(key):
    total = SEQS * SEQ_LEN
    shortest = max(SEQ_LEN * 2 // 5, 1)
    longest = SEQ_LEN * 4
    count = total // shortest + 2
    doc_lengths = jax.random.randint(jax.random.fold_in(key, 11), (count,), shortest, longest + 1).astype(jnp.int32)
    doc_lengths = doc_lengths.at[0].set(SEQ_LEN + 1)
    doc_lengths = doc_lengths.at[1].set(shortest)
    doc_lengths = doc_lengths.at[2].set(shortest)
    doc_lengths = doc_lengths.at[3].set(shortest)
    doc_lengths = doc_lengths.at[4].set(longest)
    doc_ends = jnp.cumsum(doc_lengths).astype(jnp.int32)
    doc_starts = (doc_ends - doc_lengths).astype(jnp.int32)
    places = jnp.arange(total, dtype=jnp.int32)
    documents = jnp.searchsorted(doc_ends, places, side='right').astype(jnp.int32)
    offsets = (places - doc_starts[documents]).astype(jnp.int32)
    grid = documents.reshape(SEQS, SEQ_LEN)
    document_segments = (grid - grid[:, :1]).astype(jnp.int32)
    return (document_segments, offsets.reshape(SEQS, SEQ_LEN))


def draw_segment_ids(key, part):
    return packing(key)[0]


def draw_positions(key, part):
    return packing(key)[1]


def spiked(entries, own_key, source, target, blocks, factor):
    owner, partner = [(jnp.arange(entries.shape[dim]) // (entries.shape[dim] // blocks)).reshape([-1 if axis == dim else 1 for axis in range(entries.ndim)]) for dim in (source, target)]
    chosen = jax.random.permutation(own_key, blocks)[partner]
    strong = (owner == chosen) | (owner == (partner + blocks // 2) % blocks)
    return jnp.where(strong, factor * entries, entries)


def level_of(rng, dims, pieces, smallest, top_value):
    factor_of, own = 1.0, jax.random.fold_in(rng, 6)
    for dim, parts in pieces:
        heights = jnp.exp(jax.random.uniform(jax.random.fold_in(own, dim), (parts,), jnp.float32, smallest / len(pieces), top_value / len(pieces)))
        factor_of = factor_of * jnp.repeat(heights, dims[dim] // parts).reshape([-1 if axis == dim else 1 for axis in range(len(dims))])
    return factor_of


def bell_draw(stream_key, extent, scale, reach, cuts=(), kind=jnp.bfloat16):
    values = scale * jax.random.normal(stream_key, extent, jnp.float32)
    if cuts:
        values = values * level_of(stream_key, extent, cuts, -0.22, 0.18)
    return jnp.clip(values, -reach, reach).astype(kind)


def noise_with(own_key, dims, spread, most, shards, heavy, kind=jnp.bfloat16):
    values = spread * jax.random.normal(own_key, dims, jnp.float32)
    if shards:
        values = values * level_of(own_key, dims, shards, -0.22, 0.18)
    return jnp.clip(spiked(values, jax.random.fold_in(own_key, 3), *heavy), -most, most).astype(kind)


def setup_inputs(seed: int = 0) -> dict:
    key_list = jax.random.split(jax.random.key(seed), 14)
    block_in = noise_with(key_list[0], (SEQS, SEQ_LEN, MODEL_WIDTH), 1.0, 6.0, ((0, 16),), (0, 2, 16, 2.0))
    cotangent = noise_with(key_list[1], (SEQS, SEQ_LEN, MODEL_WIDTH), 1.0, 6.0, ((0, 16),), (0, 2, 16, 2.0))
    segment_ids = draw_segment_ids(jax.random.fold_in(key_list[13], 71), 0)
    positions = draw_positions(jax.random.fold_in(key_list[13], 71), 0)
    norm1_gain = jnp.clip(1.0 + 0.1 * jax.random.normal(key_list[4], (MODEL_WIDTH,), jnp.float32), 0.5, 1.5).astype(jnp.bfloat16)
    norm2_gain = jnp.clip(1.0 + 0.1 * jax.random.normal(key_list[5], (MODEL_WIDTH,), jnp.float32), 0.5, 1.5).astype(jnp.bfloat16)
    w_query = bell_draw(key_list[6], (MODEL_WIDTH, NH * HEAD_SIZE), MODEL_WIDTH ** -0.5, 0.15625, ((0, 16), (1, 2)))
    key_projection = bell_draw(key_list[7], (MODEL_WIDTH, KEY_VALUE_HEADS * HEAD_SIZE), MODEL_WIDTH ** -0.5, 0.15625, ((0, 16), (1, 2)))
    value_projection = bell_draw(key_list[8], (MODEL_WIDTH, KEY_VALUE_HEADS * HEAD_SIZE), MODEL_WIDTH ** -0.5, 0.15625, ((0, 16), (1, 2)))
    w_out = bell_draw(key_list[9], (NH * HEAD_SIZE, MODEL_WIDTH), HEAD_SIZE ** -0.5, 0.625, ((0, 2), (1, 16)))
    w_gate = bell_draw(key_list[10], (MODEL_WIDTH, FF), MODEL_WIDTH ** -0.5, 0.15625, ((0, 16), (1, 2)))
    w_up = bell_draw(key_list[11], (MODEL_WIDTH, FF), MODEL_WIDTH ** -0.5, 0.15625, ((0, 16), (1, 2)))
    w_down = bell_draw(key_list[12], (FF, MODEL_WIDTH), FF ** -0.5, 0.09375, ((0, 2), (1, 16)))
    return dict(block_in=block_in, cotangent=cotangent, segment_ids=segment_ids, positions=positions, norm1_gain=norm1_gain, norm2_gain=norm2_gain, w_query=w_query, key_projection=key_projection, value_projection=value_projection, w_out=w_out, w_gate=w_gate, w_up=w_up, w_down=w_down)


EPS = 1e-05
ROPE_BASE = 10000.0

def inv_rms(values):
    return lax.rsqrt(lax.optimization_barrier(jnp.mean(values * values, -1, keepdims=True)) + EPS)

def norm_back(grad_out, values, scale_row, gain):
    normed = values * scale_row
    scaled = grad_out * gain
    back = scale_row * (scaled - normed * lax.optimization_barrier(jnp.mean(scaled * normed, -1, keepdims=True)))
    return (back, lax.optimization_barrier(jnp.sum(grad_out * normed, 0)))

def rotary_tables(positions, width):
    half = width // 2
    freqs = jnp.exp(-math.log(ROPE_BASE) * (2.0 * jnp.arange(half, dtype=jnp.float32)) / width)
    angles = positions.astype(jnp.float32)[:, None] * freqs[None, :]
    return (jnp.cos(angles)[:, None, :], jnp.sin(angles)[:, None, :])

def rotate(values, cosines, sines):
    half = values.shape[-1] // 2
    first, second = (values[..., :half], values[..., half:])
    return jnp.concatenate([first * cosines - second * sines, second * cosines + first * sines], -1)

def inverse_rotation(grads, cosines, sines):
    half = grads.shape[-1] // 2
    first, second = (grads[..., :half], grads[..., half:])
    return jnp.concatenate([first * cosines + second * sines, second * cosines - first * sines], -1)

def seq_mask(document_segments):
    index = jnp.arange(document_segments.shape[0])
    return (document_segments[:, None] == document_segments[None, :]) & (index[:, None] >= index[None, :])

def scores_of(query, key_block, mask):
    raw = jnp.einsum('qhgd,khd->hgqk', query.astype(jnp.float32), key_block.astype(jnp.float32)) * HEAD_SIZE ** (-0.5)
    return jnp.where(mask[None, None], raw, -1e+30)

def attend_one(query, key_block, value_block, document_segments):
    mask = seq_mask(document_segments)
    scores = scores_of(query, key_block, mask)
    highest = lax.optimization_barrier(jnp.max(scores, -1, keepdims=True))
    log_total = highest + jnp.log(lax.optimization_barrier(jnp.sum(jnp.exp(scores - highest), -1, keepdims=True)))
    probs = jnp.exp(scores - log_total).astype(jnp.bfloat16)
    attended = jnp.einsum('hgqk,khd->qhgd', probs.astype(jnp.float32), value_block.astype(jnp.float32))
    return (attended.astype(jnp.bfloat16), log_total)

def attend_back(query, key_block, value_block, done, grad_done, log_total, document_segments):
    mask = seq_mask(document_segments)
    scores = scores_of(query, key_block, mask)
    probs = jnp.where(mask[None, None], jnp.exp(scores - log_total), 0.0)
    grad_f = grad_done.astype(jnp.float32)
    grad_probs = jnp.einsum('qhgd,khd->hgqk', grad_f, value_block.astype(jnp.float32))
    row_dots = jnp.einsum('qhgd,qhgd->hgq', grad_f, done.astype(jnp.float32))[..., None]
    grad_scores = probs * (grad_probs - row_dots)
    grad_value = jnp.einsum('hgqk,qhgd->khd', probs.astype(jnp.bfloat16).astype(jnp.float32), grad_f)
    grad_sb = grad_scores.astype(jnp.bfloat16).astype(jnp.float32)
    grad_query = jnp.einsum('hgqk,khd->qhgd', grad_sb, key_block.astype(jnp.float32)) * HEAD_SIZE ** (-0.5)
    grad_key = jnp.einsum('hgqk,qhgd->khd', grad_sb, query.astype(jnp.float32)) * HEAD_SIZE ** (-0.5)
    return (grad_query, grad_key, grad_value)

def block_pass(block_in, cotangent, segment_ids, positions, norm1_gain, norm2_gain, w_query, key_projection, value_projection, w_out, w_gate, w_up, w_down):
    seqs, length, width = block_in.shape
    rows = seqs * length
    heads = w_query.shape[1] // HEAD_SIZE
    kv_heads = key_projection.shape[1] // HEAD_SIZE
    group = heads // kv_heads
    inputs = block_in.reshape(rows, width).astype(jnp.float32)
    gain_one = norm1_gain.astype(jnp.float32)
    gain_two = norm2_gain.astype(jnp.float32)
    scale_one = inv_rms(inputs)
    normed_one = (inputs * scale_one * gain_one).astype(jnp.bfloat16)
    cosines, sines = rotary_tables(positions.reshape(rows), HEAD_SIZE)
    queries = rotate(jnp.dot(normed_one, w_query, preferred_element_type=jnp.float32).reshape(rows, heads, HEAD_SIZE), cosines, sines).astype(jnp.bfloat16)
    keys = rotate(jnp.dot(normed_one, key_projection, preferred_element_type=jnp.float32).reshape(rows, kv_heads, HEAD_SIZE), cosines, sines).astype(jnp.bfloat16)
    values = jnp.dot(normed_one, value_projection, preferred_element_type=jnp.float32).astype(jnp.bfloat16)
    query_seq = queries.reshape(seqs, length, kv_heads, group, HEAD_SIZE)
    key_seq = keys.reshape(seqs, length, kv_heads, HEAD_SIZE)
    value_seq = values.reshape(seqs, length, kv_heads, HEAD_SIZE)
    attended, log_totals = jax.vmap(attend_one)(query_seq, key_seq, value_seq, segment_ids)
    attended_rows = attended.reshape(rows, heads * HEAD_SIZE)
    mixed = inputs + jnp.dot(attended_rows, w_out, preferred_element_type=jnp.float32)
    scale_two = inv_rms(mixed)
    normed_two = (mixed * scale_two * gain_two).astype(jnp.bfloat16)
    gate = jnp.dot(normed_two, w_gate, preferred_element_type=jnp.float32)
    up_proj = jnp.dot(normed_two, w_up, preferred_element_type=jnp.float32)
    sigma = jax.nn.sigmoid(gate)
    hidden = (gate * sigma * up_proj).astype(jnp.bfloat16)
    output = (mixed + jnp.dot(hidden, w_down, preferred_element_type=jnp.float32)).astype(jnp.bfloat16)
    grad_rows = cotangent.reshape(rows, width)
    grad_down = jnp.dot(hidden.T, grad_rows, preferred_element_type=jnp.float32)
    grad_hidden = jnp.dot(grad_rows, w_down.T, preferred_element_type=jnp.float32)
    grad_upin = (grad_hidden * gate * sigma).astype(jnp.bfloat16)
    grad_gatein = (grad_hidden * up_proj * sigma * (1.0 + gate * (1.0 - sigma))).astype(jnp.bfloat16)
    grad_gate = jnp.dot(normed_two.T, grad_gatein, preferred_element_type=jnp.float32)
    grad_up = jnp.dot(normed_two.T, grad_upin, preferred_element_type=jnp.float32)
    grad_normed_two = jnp.dot(grad_gatein, w_gate.T, preferred_element_type=jnp.float32) + jnp.dot(grad_upin, w_up.T, preferred_element_type=jnp.float32)
    back_two, grad_gain_two = norm_back(grad_normed_two, mixed, scale_two, gain_two)
    grad_mixed = grad_rows.astype(jnp.float32) + back_two
    grad_mixedb = grad_mixed.astype(jnp.bfloat16)
    grad_outw = jnp.dot(attended_rows.T, grad_mixedb, preferred_element_type=jnp.float32)
    grad_attended = jnp.dot(grad_mixedb, w_out.T, preferred_element_type=jnp.float32).astype(jnp.bfloat16)
    grad_seq = grad_attended.reshape(seqs, length, kv_heads, group, HEAD_SIZE)
    grad_q, grad_k, grad_v = jax.vmap(attend_back)(query_seq, key_seq, value_seq, attended, grad_seq, log_totals, segment_ids)
    grad_qin = inverse_rotation(grad_q.reshape(rows, heads, HEAD_SIZE), cosines, sines).reshape(rows, heads * HEAD_SIZE).astype(jnp.bfloat16)
    grad_kin = inverse_rotation(grad_k.reshape(rows, kv_heads, HEAD_SIZE), cosines, sines).reshape(rows, kv_heads * HEAD_SIZE).astype(jnp.bfloat16)
    grad_vin = grad_v.reshape(rows, kv_heads * HEAD_SIZE).astype(jnp.bfloat16)
    grad_queryw = jnp.dot(normed_one.T, grad_qin, preferred_element_type=jnp.float32)
    key_weight_gradient = jnp.dot(normed_one.T, grad_kin, preferred_element_type=jnp.float32)
    grad_valuew = jnp.dot(normed_one.T, grad_vin, preferred_element_type=jnp.float32)
    grad_normed_one = jnp.dot(grad_qin, w_query.T, preferred_element_type=jnp.float32) + jnp.dot(grad_kin, key_projection.T, preferred_element_type=jnp.float32) + jnp.dot(grad_vin, value_projection.T, preferred_element_type=jnp.float32)
    back_one, grad_gain_one = norm_back(grad_normed_one, inputs, scale_one, gain_one)
    grad_input = grad_mixed + back_one
    grads = (grad_gain_one, grad_gain_two, grad_queryw, key_weight_gradient, grad_valuew, grad_outw, grad_gate, grad_up, grad_down)
    return (output.reshape(seqs, length, width), grad_input.reshape(seqs, length, width), grads)

def reference(block_in, cotangent, segment_ids, positions, norm1_gain, norm2_gain, w_query, key_projection, value_projection, w_out, w_gate, w_up, w_down):
    blocks = block_in.shape[0] // SEQ_DEV
    weights = (norm1_gain, norm2_gain, w_query, key_projection, value_projection, w_out, w_gate, w_up, w_down)

    def split(array):
        return array.reshape((blocks, SEQ_DEV) + array.shape[1:])
    zeros = tuple((jnp.zeros(weight.shape, jnp.float32) for weight in weights))

    def step(totals, item):
        output, grad_input, grads = block_pass(item[0], item[1], item[2], item[3], *weights)
        return (tuple((total + grad for total, grad in zip(totals, grads))), (output, grad_input))
    totals, (outputs, grad_inputs) = lax.scan(step, zeros, (split(block_in), split(cotangent), split(segment_ids), split(positions)))
    return (outputs.reshape(block_in.shape), grad_inputs.reshape(block_in.shape), totals[0], totals[1], totals[2], totals[3], totals[4], totals[5], totals[6], totals[7], totals[8])
```

```python
import functools
import math

import jax
import jax.numpy as jnp
from jax import lax
from jax.experimental import pallas as pl
from jax.experimental.pallas import tpu as pltpu
from jax.sharding import PartitionSpec as P

HEAD_SIZE = 96
EPS = 1e-05
ROPE_BASE = 10000.0
LANES = 128
NEG = -1e30
SCALE = HEAD_SIZE ** (-0.5)
BF16 = jnp.bfloat16
F32 = jnp.float32


def matmul(left, right):
    return jnp.dot(left, right, preferred_element_type=F32)


def matmul_tn(left, right):
    return lax.dot_general(left, right, (((0,), (0,)), ((), ())), preferred_element_type=F32)


def matmul_nt(left, right):
    return lax.dot_general(left, right, (((1,), (1,)), ((), ())), preferred_element_type=F32)


def inv_rms(values):
    return lax.rsqrt(jnp.mean(values * values, -1, keepdims=True) + EPS)


def factors_of(count):
    out = []
    while count > 4 and count % 4 == 0:
        out.append(4)
        count //= 4
    while count > 1 and count % 2 == 0:
        out.append(2)
        count //= 2
    if count > 1:
        out.append(count)
    return out


class Ring:
    def __init__(self, count):
        self.count = count
        self.factors = factors_of(count)
        self.strides = []
        stride = count
        for f in self.factors:
            stride //= f
            self.strides.append(stride)

    def digit(self, axis):
        return (lax.axis_index("dp") // self.strides[axis]) % self.factors[axis]

    def shift(self, axis, k):
        f, s = self.factors[axis], self.strides[axis]
        pairs = []
        for i in range(self.count):
            d = (i // s) % f
            pairs.append((i, i + (((d + k) % f) - d) * s))
        return pairs

    def send(self, value, axis, k):
        return lax.ppermute(value, "dp", self.shift(axis, k))

    def gather(self, shard):
        parts = [(shard, ())]
        for axis in range(len(self.factors)):
            more = [(p, steps + (0,)) for p, steps in parts]
            for k in range(1, self.factors[axis]):
                for p, steps in parts:
                    more.append((self.send(p, axis, k), steps + (k,)))
            parts = more
        return [p for p, _ in parts], [s for _, s in parts]

    def places(self, steps):
        out = []
        for st in steps:
            place = 0
            for axis, k in enumerate(st):
                f = self.factors[axis]
                place = place + ((self.digit(axis) + f - k) % f) * self.strides[axis]
            out.append(place)
        return jnp.stack([jnp.asarray(p, jnp.int32) for p in out])

    def scatter(self, grad, final=F32):
        cur = grad.reshape(tuple(self.factors) + grad.shape[1:])
        for axis in reversed(range(len(self.factors))):
            f = self.factors[axis]
            d = self.digit(axis)
            kind = final if axis == 0 else BF16
            got = []
            for k in range(1, f):
                out = lax.dynamic_index_in_dim(cur, (d + k) % f, axis, keepdims=False)
                got.append(self.send(out, axis, k))
            total = lax.dynamic_index_in_dim(cur, d, axis, keepdims=False).astype(F32)
            for g in got:
                total = total + g.astype(F32)
            cur = total.astype(kind)
        return cur


def assemble_body(places, *refs):
    out = refs[-1]
    for i, ref in enumerate(refs[:-1]):
        out[places[i]] = ref[...]


def assemble(parts, places):
    count = len(parts)
    r, w = parts[0].shape
    bw = w
    for cand in (512, 384, 256, 128):
        if w % cand == 0:
            bw = cand
            break
    out = pl.pallas_call(
        assemble_body,
        grid_spec=pltpu.PrefetchScalarGridSpec(
            num_scalar_prefetch=1,
            grid=(w // bw,),
            in_specs=[pl.BlockSpec((r, bw), lambda j, s: (0, j))] * count,
            out_specs=pl.BlockSpec((count, r, bw), lambda j, s: (0, 0, j)),
        ),
        out_shape=jax.ShapeDtypeStruct((count, r, w), parts[0].dtype),
        cost_estimate=pl.CostEstimate(flops=0, bytes_accessed=4 * count * r * w, transcendentals=0),
        name="assemble",
    )(places, *parts)
    return out.reshape(count * r, w)


def exchange(partial, size):
    total = partial.astype(F32)
    for k in range(1, size):
        pairs = [(i, (i + k) % size) for i in range(size)]
        total = total + lax.ppermute(partial, "tensor", pairs).astype(F32)
    return total


def unpack(cols, lane):
    c0, c1, c2 = (cols[:, i * LANES : (i + 1) * LANES] for i in range(3))
    heads = (
        c0,
        pltpu.roll(jnp.where(lane >= 96, c0, c1), 32, 1),
        pltpu.roll(jnp.where(lane >= 64, c1, c2), 64, 1),
        pltpu.roll(c2, 96, 1),
    )
    return [jnp.where(lane < HEAD_SIZE, h, 0.0) for h in heads]


def pack(heads, lane):
    a, b, c, d = heads
    b, c, d = pltpu.roll(b, 96, 1), pltpu.roll(c, 64, 1), pltpu.roll(d, 32, 1)
    return jnp.concatenate(
        [
            jnp.where(lane < 96, a, b),
            jnp.where(lane < 64, b, c),
            jnp.where(lane < 32, c, d),
        ],
        1,
    )


def partner(x, lane):
    return jnp.where(lane < HEAD_SIZE // 2, pltpu.roll(x, 80, 1), pltpu.roll(x, 48, 1))


def fill_bias(bias_ref, segc_ref, segr_ref):
    length = bias_ref.shape[0]
    row = lax.broadcasted_iota(jnp.int32, (length, length), 0)
    col = lax.broadcasted_iota(jnp.int32, (length, length), 1)
    keep = (segc_ref[0] == segr_ref[0]) & (row >= col)
    bias_ref[...] = jnp.where(keep, 0.0, NEG)


def forward_kernel(kv_heads, block, qkv_ref, cos_ref, sin_ref, segc_ref, segr_ref, heads_ref, att_ref, lse_ref, bias_ref):
    length = bias_ref.shape[0]
    lane = lax.broadcasted_iota(jnp.int32, (length, LANES), 1)
    fill_bias(bias_ref, segc_ref, segr_ref)
    cos, sin = cos_ref[...], sin_ref[...]
    group = 2
    heads = kv_heads * group
    width = 4 * HEAD_SIZE
    for part in range(heads // 4):
        for i, h in enumerate(unpack(qkv_ref[:, part * width : (part + 1) * width], lane)):
            heads_ref[0, part * 4 + i] = (h * cos + partner(h, lane) * sin).astype(BF16)
    koff, voff = heads * HEAD_SIZE, (heads + kv_heads) * HEAD_SIZE
    for part in range(kv_heads // 4):
        for i, h in enumerate(unpack(qkv_ref[:, koff + part * width : koff + (part + 1) * width], lane)):
            heads_ref[0, heads + part * 4 + i] = (h * cos + partner(h, lane) * sin).astype(BF16)
        for i, h in enumerate(unpack(qkv_ref[:, voff + part * width : voff + (part + 1) * width], lane)):
            heads_ref[0, heads + kv_heads + part * 4 + i] = h.astype(BF16)
    small = lane[:block]
    for b in range(length // block):
        lo, end = b * block, (b + 1) * block
        bias = bias_ref[lo:end, :end]
        bias = jnp.concatenate([bias] * group, 0)
        lse_all = jnp.zeros((block, LANES), F32)
        done = []
        for g in range(kv_heads):
            q = jnp.concatenate([heads_ref[0, g * group + i, lo:end, :] for i in range(group)], 0)
            k = heads_ref[0, heads + g, :end, :]
            v = heads_ref[0, heads + kv_heads + g, :end, :]
            s = lax.dot_general(q, k, (((1,), (1,)), ((), ())), preferred_element_type=F32) + bias
            m = jnp.max(s, -1, keepdims=True)
            p = jnp.exp((s - m) * SCALE)
            total = jnp.sum(p, -1, keepdims=True)
            lse = m * SCALE + jnp.log(total)
            p = (p * (1.0 / total)).astype(BF16)
            o = jnp.dot(p, v, preferred_element_type=F32)
            for i in range(group):
                done.append(o[i * block : (i + 1) * block])
                lse_all = jnp.where(small == g * group + i, lse[i * block : (i + 1) * block], lse_all)
        lse_ref[lo:end, :] = lse_all
        for part in range(heads // 4):
            att_ref[lo:end, part * width : (part + 1) * width] = pack(done[part * 4 : part * 4 + 4], small).astype(BF16)


def backward_kernel(kv_heads, block, heads_ref, att_ref, gatt_ref, lse_ref, cos_ref, sin_ref, segc_ref, segr_ref, out_ref, bias_ref, dout_ref, dot_ref):
    length = bias_ref.shape[0]
    lane = lax.broadcasted_iota(jnp.int32, (length, LANES), 1)
    fill_bias(bias_ref, segc_ref, segr_ref)
    cos, sin = cos_ref[...], sin_ref[...]
    group = 2
    heads = kv_heads * group
    width = 4 * HEAD_SIZE
    rowdot = jnp.zeros((length, LANES), F32)
    for part in range(heads // 4):
        done = unpack(att_ref[:, part * width : (part + 1) * width].astype(F32), lane)
        gdone = unpack(gatt_ref[:, part * width : (part + 1) * width].astype(F32), lane)
        for i in range(4):
            dout_ref[part * 4 + i] = gdone[i].astype(BF16)
            rowdot = jnp.where(lane == part * 4 + i, jnp.sum(done[i] * gdone[i], -1, keepdims=True), rowdot)
    dot_ref[...] = rowdot
    nt = (((1,), (1,)), ((), ()))
    tn = (((0,), (0,)), ((), ()))
    dqs, dks, dvs = [], [], []
    for g in range(kv_heads):
        dq_blocks = []
        dk = dv = None
        for b in reversed(range(length // block)):
            lo, end = b * block, (b + 1) * block
            q = jnp.concatenate([heads_ref[0, g * group + i, lo:end, :] for i in range(group)], 0)
            do = jnp.concatenate([dout_ref[g * group + i, lo:end, :] for i in range(group)], 0)
            lse = jnp.concatenate([lse_ref[lo:end, g * group + i : g * group + i + 1] for i in range(group)], 0)
            rd = jnp.concatenate([dot_ref[lo:end, g * group + i : g * group + i + 1] for i in range(group)], 0)
            bias = bias_ref[lo:end, :end]
            bias = jnp.concatenate([bias] * group, 0)
            k = heads_ref[0, heads + g, :end, :]
            v = heads_ref[0, heads + kv_heads + g, :end, :]
            s = lax.dot_general(q, k, nt, preferred_element_type=F32)
            p = jnp.exp(s * SCALE + (bias - lse))
            dp = lax.dot_general(do, v, nt, preferred_element_type=F32)
            ds = (p * (dp - rd)).astype(BF16)
            p = p.astype(BF16)
            dvb = lax.dot_general(p, do, tn, preferred_element_type=F32)
            dkb = lax.dot_general(ds, q, tn, preferred_element_type=F32)
            dqb = jnp.dot(ds, k, preferred_element_type=F32)
            dq_blocks.insert(0, dqb)
            if dk is None:
                dk, dv = dkb, dvb
            else:
                dk = jnp.concatenate([dk[:end] + dkb, dk[end:]], 0)
                dv = jnp.concatenate([dv[:end] + dvb, dv[end:]], 0)
        for i in range(group):
            dq = jnp.concatenate([x[i * block : (i + 1) * block] for x in dq_blocks], 0) * SCALE
            dqs.append(dq * cos - partner(dq, lane) * sin)
        dk = dk * SCALE
        dks.append(dk * cos - partner(dk, lane) * sin)
        dvs.append(dv)
        if len(dqs) == 4:
            at = (g // 2) * width
            out_ref[:, at : at + width] = pack(dqs, lane).astype(BF16)
            dqs = []
    koff, voff = heads * HEAD_SIZE, (heads + kv_heads) * HEAD_SIZE
    for part in range(kv_heads // 4):
        out_ref[:, koff + part * width : koff + (part + 1) * width] = pack(dks[part * 4 : part * 4 + 4], lane).astype(BF16)
        out_ref[:, voff + part * width : voff + (part + 1) * width] = pack(dvs[part * 4 : part * 4 + 4], lane).astype(BF16)


def attention_forward(qkv, cos, sin, segc, segr, kv_heads, length):
    rows, wide = qkv.shape
    seqs = rows // length
    heads = 2 * kv_heads
    row = lambda s: (s, 0)
    return pl.pallas_call(
        functools.partial(forward_kernel, kv_heads, 256),
        grid=(seqs,),
        in_specs=[
            pl.BlockSpec((length, wide), row),
            pl.BlockSpec((length, LANES), row),
            pl.BlockSpec((length, LANES), row),
            pl.BlockSpec((1, length, 1), lambda s: (s, 0, 0)),
            pl.BlockSpec((1, 1, length), lambda s: (s, 0, 0)),
        ],
        out_specs=[
            pl.BlockSpec((1, heads + 2 * kv_heads, length, LANES), lambda s: (s, 0, 0, 0)),
            pl.BlockSpec((length, heads * HEAD_SIZE), row),
            pl.BlockSpec((length, LANES), row),
        ],
        out_shape=[
            jax.ShapeDtypeStruct((seqs, heads + 2 * kv_heads, length, LANES), BF16),
            jax.ShapeDtypeStruct((rows, heads * HEAD_SIZE), BF16),
            jax.ShapeDtypeStruct((rows, LANES), F32),
        ],
        scratch_shapes=[pltpu.VMEM((length, length), F32)],
        cost_estimate=pl.CostEstimate(
            flops=8 * seqs * heads * length * length * LANES,
            bytes_accessed=10 * rows * wide,
            transcendentals=seqs * heads * length * length,
        ),
        name="attention_forward",
    )(qkv, cos, sin, segc, segr)


def attention_backward(heads_kept, att, gatt, lse, cos, sin, segc, segr, kv_heads, length):
    rows = att.shape[0]
    seqs = rows // length
    heads = 2 * kv_heads
    wide = (heads + 2 * kv_heads) * HEAD_SIZE
    row = lambda s: (s, 0)
    return pl.pallas_call(
        functools.partial(backward_kernel, kv_heads, 256),
        grid=(seqs,),
        in_specs=[
            pl.BlockSpec((1, heads + 2 * kv_heads, length, LANES), lambda s: (s, 0, 0, 0)),
            pl.BlockSpec((length, heads * HEAD_SIZE), row),
            pl.BlockSpec((length, heads * HEAD_SIZE), row),
            pl.BlockSpec((length, LANES), row),
            pl.BlockSpec((length, LANES), row),
            pl.BlockSpec((length, LANES), row),
            pl.BlockSpec((1, length, 1), lambda s: (s, 0, 0)),
            pl.BlockSpec((1, 1, length), lambda s: (s, 0, 0)),
        ],
        out_specs=pl.BlockSpec((length, wide), row),
        out_shape=jax.ShapeDtypeStruct((rows, wide), BF16),
        scratch_shapes=[
            pltpu.VMEM((length, length), F32),
            pltpu.VMEM((heads, length, LANES), BF16),
            pltpu.VMEM((length, LANES), F32),
        ],
        cost_estimate=pl.CostEstimate(
            flops=20 * seqs * heads * length * length * LANES,
            bytes_accessed=10 * rows * wide,
            transcendentals=seqs * heads * length * length,
        ),
        name="attention_backward",
    )(heads_kept, att, gatt, lse, cos, sin, segc, segr)


def hidden_kernel(n_ref, c_ref, wgu_ref, wd_ref, hid_ref, ggu_ref):
    tile = hid_ref.shape[1]
    gu = jnp.dot(n_ref[...], wgu_ref[...], preferred_element_type=F32)
    gh = jnp.dot(c_ref[...], wd_ref[...], preferred_element_type=F32)
    gate, up = gu[:, :tile], gu[:, tile:]
    sig = jax.nn.sigmoid(gate)
    act = gate * sig
    hid_ref[...] = (act * up).astype(BF16)
    ggu_ref[:, tile:] = (gh * act).astype(BF16)
    ggu_ref[:, :tile] = (gh * up * sig * (1.0 + gate * (1.0 - sig))).astype(BF16)


def hidden_pass(normed, cot, wgu, wdown, tile):
    rows, d = normed.shape
    h = wdown.shape[1]
    return pl.pallas_call(
        hidden_kernel,
        grid=(h // tile,),
        in_specs=[
            pl.BlockSpec((rows, d), lambda j: (0, 0)),
            pl.BlockSpec((rows, d), lambda j: (0, 0)),
            pl.BlockSpec((d, 2 * tile), lambda j: (0, j)),
            pl.BlockSpec((d, tile), lambda j: (0, j)),
        ],
        out_specs=[
            pl.BlockSpec((rows, tile), lambda j: (0, j)),
            pl.BlockSpec((rows, 2 * tile), lambda j: (0, j)),
        ],
        out_shape=[
            jax.ShapeDtypeStruct((rows, h), BF16),
            jax.ShapeDtypeStruct((rows, 2 * h), BF16),
        ],
        cost_estimate=pl.CostEstimate(
            flops=6 * rows * d * h, bytes_accessed=6 * d * h + 4 * rows * d + 6 * rows * h, transcendentals=rows * h
        ),
        name="hidden_pass",
    )(normed, cot, wgu, wdown)


def interleave(gate, up, tile):
    r, h = gate.shape
    both = jnp.stack([gate.reshape(r, h // tile, tile), up.reshape(r, h // tile, tile)], 2)
    return both.reshape(r, 2 * h)


def deinterleave(both, tile):
    r, wide = both.shape
    both = both.reshape(r, wide // (2 * tile), 2, tile)
    return both[:, :, 0].reshape(r, wide // 2), both[:, :, 1].reshape(r, wide // 2)


def rotary(positions):
    half = HEAD_SIZE // 2
    freqs = jnp.exp(-math.log(ROPE_BASE) * (2.0 * jnp.arange(half, dtype=F32)) / HEAD_SIZE)
    angles = positions.astype(F32)[:, None] * freqs[None, :]
    cos, sin = jnp.cos(angles), jnp.sin(angles)
    zero = jnp.zeros((positions.shape[0], LANES - HEAD_SIZE), F32)
    return jnp.concatenate([cos, cos, zero], 1), jnp.concatenate([-sin, sin, zero], 1)


def norm_back(grad_out, normed, scale_row, gain):
    scaled = grad_out * gain
    return scale_row * (scaled - normed * jnp.mean(scaled * normed, -1, keepdims=True))


def per_device(
    sizes,
    block_in,
    cotangent,
    segment_ids,
    positions,
    norm1_gain,
    norm2_gain,
    w_query,
    key_projection,
    value_projection,
    w_out,
    w_gate,
    w_up,
    w_down,
):
    ring = Ring(sizes["dp"])
    tensor = sizes["tensor"]
    count = ring.count
    seqs, length, width = block_in.shape
    rows = seqs * length
    qw, kw = w_query.shape[1], key_projection.shape[1]
    hid = w_gate.shape[1]
    kv_heads = kw // HEAD_SIZE
    tile = 256 if hid % 256 == 0 else hid
    share = norm1_gain.shape[0]

    gains = jnp.stack([norm1_gain, norm2_gain])
    wqkv = jnp.concatenate([w_query, key_projection, value_projection], 1)
    wot = w_out.T
    wgu = interleave(w_gate, w_up, tile)
    wdt = w_down.T

    gain_parts, steps = ring.gather(gains)
    qkv_parts, _ = ring.gather(wqkv)
    out_parts, _ = ring.gather(wot)
    gu_parts, _ = ring.gather(wgu)
    down_parts, _ = ring.gather(wdt)
    places = ring.places(steps)

    order = jnp.zeros((count,), jnp.int32).at[places].set(jnp.arange(count, dtype=jnp.int32))
    gain_all = jnp.stack(gain_parts)[order].astype(F32)
    gain_one = gain_all[:, 0].reshape(1, width)
    gain_two = gain_all[:, 1].reshape(1, width)

    cos, sin = rotary(positions.reshape(rows))
    segc, segr = segment_ids[:, :, None], segment_ids[:, None, :]
    inputs = block_in.reshape(rows, width).astype(F32)
    scale_one = inv_rms(inputs)
    normed_one = (inputs * scale_one * gain_one).astype(BF16)
    cot_rows = cotangent.reshape(rows, width)

    qkv_full = assemble(qkv_parts, places)
    qkv = matmul(normed_one, qkv_full)
    kept, attended, lse = attention_forward(qkv, cos, sin, segc, segr, kv_heads, length)
    out_full = assemble(out_parts, places)

    span = [slice(i * length, (i + 1) * length) for i in range(seqs)]
    mixed = []
    for s in span:
        part = matmul_nt(attended[s], out_full).astype(BF16)
        mixed.append(inputs[s] + exchange(part, tensor))
    gu_full = assemble(gu_parts, places)
    down_full = assemble(down_parts, places)
    scale_two = [inv_rms(m) for m in mixed]
    normed_two = [(m * r * gain_two).astype(BF16) for m, r in zip(mixed, scale_two)]
    hiddens, ggus, outputs, gn2 = [], [], [], []
    for i, s in enumerate(span):
        h, ggu = hidden_pass(normed_two[i], cot_rows[s], gu_full, down_full, tile)
        hiddens.append(h)
        ggus.append(ggu)
        part = matmul_nt(ggu, gu_full).astype(BF16)
        gn2.append(exchange(part, tensor))
    for i, s in enumerate(span):
        part = matmul_nt(hiddens[i], down_full).astype(BF16)
        outputs.append((mixed[i] + exchange(part, tensor)).astype(BF16))

    hidden_all = jnp.concatenate(hiddens, 0)
    ggu_all = jnp.concatenate(ggus, 0)
    n2_all = jnp.concatenate(normed_two, 0)
    grad_down = matmul_tn(cot_rows, hidden_all).astype(BF16)
    down_shard = ring.scatter(grad_down.reshape(count, share, hid))
    grad_gu = matmul_tn(n2_all, ggu_all).astype(BF16)
    gu_shard = ring.scatter(grad_gu.reshape(count, share, 2 * hid))

    grad_mixed, grad_att = [], []
    gain2 = 0.0
    for i, s in enumerate(span):
        normed = mixed[i] * scale_two[i]
        gain2 = gain2 + jnp.sum(gn2[i] * normed, 0)
        back = norm_back(gn2[i], normed, scale_two[i], gain_two)
        gm = cot_rows[s].astype(F32) + back
        grad_mixed.append(gm)
        grad_att.append(matmul(gm.astype(BF16), out_full).astype(BF16))
    gm_b = jnp.concatenate([g.astype(BF16) for g in grad_mixed], 0)
    grad_out = matmul_tn(gm_b, attended).astype(BF16)
    out_shard = ring.scatter(grad_out.reshape(count, share, qw))

    gin = []
    for i, s in enumerate(span):
        gin.append(
            attention_backward(
                kept[i : i + 1], attended[s], grad_att[i], lse[s], cos[s], sin[s],
                segc[i : i + 1], segr[i : i + 1], kv_heads, length,
            )
        )
    gin_all = jnp.concatenate(gin, 0)
    grad_qkv = matmul_tn(normed_one, gin_all).astype(BF16)
    qkv_shard = ring.scatter(grad_qkv.reshape(count, share, qw + 2 * kw))

    grad_input = []
    gain1 = 0.0
    for i, s in enumerate(span):
        part = matmul_nt(gin[i], qkv_full).astype(BF16)
        gn1 = exchange(part, tensor)
        normed = inputs[s] * scale_one[s]
        gain1 = gain1 + jnp.sum(gn1 * normed, 0)
        grad_input.append(grad_mixed[i] + norm_back(gn1, normed, scale_one[s], gain_one))

    gain_grad = jnp.stack([gain1.reshape(count, share), gain2.reshape(count, share)], 1)
    gain_shard = gain_scatter(ring, gain_grad)
    gate_shard, up_shard = deinterleave(gu_shard, tile)
    return (
        jnp.stack([o.reshape(length, width) for o in outputs]),
        jnp.stack([g.reshape(length, width) for g in grad_input]),
        gain_shard[0],
        gain_shard[1],
        qkv_shard[:, :qw],
        qkv_shard[:, qw : qw + kw],
        qkv_shard[:, qw + kw :],
        out_shard.T,
        gate_shard,
        up_shard,
        down_shard.T,
    )


def gain_scatter(ring, grad):
    cur = grad.reshape(tuple(ring.factors) + grad.shape[1:])
    for axis in reversed(range(len(ring.factors))):
        f = ring.factors[axis]
        d = ring.digit(axis)
        total = lax.dynamic_index_in_dim(cur, d, axis, keepdims=False)
        for k in range(1, f):
            out = lax.dynamic_index_in_dim(cur, (d + k) % f, axis, keepdims=False)
            total = total + ring.send(out, axis, k)
        cur = total
    return cur


def solution(mesh):
    sizes = dict(mesh.shape)
    rows, both, back = P("dp", None, None), P("dp", "tensor"), P("tensor", "dp")
    in_specs = (rows, rows, P("dp", None), P("dp", None), P("dp"), P("dp"), both, both, both, back, both, both, back)
    out_specs = (rows, rows, P("dp"), P("dp"), both, both, both, back, both, both, back)
    return jax.shard_map(
        functools.partial(per_device, sizes), mesh=mesh, in_specs=in_specs, out_specs=out_specs, check_vma=False
    )
```
